128 devices in a mesh: row: 8 (over x_hi, y), col: 16 (over z, x_lo, core).
Axes of the slice: x: 4 (x_hi: 2, x_lo: 2; x = x_hi * 2 + x_lo), y: 4, z: 4, core: 2. Of those that a mesh axis runs over, the one named last changes fastest.
Arguments:
- doubles: float32 [32, 32, 192, 192], P(None, None, 'row', 'col'), may hold values from -6 to 6
- cycle_inter: float32 [6144, 6144], P('row', 'col'), may hold values from -0.078125 to 0.078125
Outputs:
- cycle_term: float32 [6144, 6144], P('row', 'col')
The draws below stay inside these ranges and needn't reach their ends.
All inputs are finite; a program needn't handle non-finite values.
Results may differ from the reference program's by a relative error of at most 0.00007.
Values sent between devices are 32-bit elements; how exact they have to be, the bound alone decides.
A program may use at most 192 MiB of HBM per device.

```python
import jax
import jax.numpy as jnp
from jax import lax

O = 32
V = 192
OV = 6144


def block_levels(stream_key, extent, split, smallest, top_value):
    def one(dim, parts):
        draws = jax.random.uniform(jax.random.fold_in(jax.random.fold_in(stream_key, 6), dim), (parts,), jnp.float32, smallest / len(split), top_value / len(split))
        return jnp.repeat(jnp.exp(draws), extent[dim] // parts).reshape((-1,) + (1,) * (len(extent) - dim - 1))

    loudness = one(*split[0])
    for cut in split[1:]:
        loudness = loudness * one(*cut)
    return loudness


def noise(own_key, shape, scale, reach, split=(), held_as=jnp.bfloat16):
    drawn = jax.random.normal(own_key, shape, jnp.float32) * scale
    if len(split) > 0:
        drawn = block_levels(own_key, shape, split, -0.22, 0.18) * drawn
    return jnp.clip(drawn, min=-reach, max=reach).astype(held_as)


def setup_inputs(seed: int = 0) -> dict:
    streams_of = jax.random.split(jax.random.key(seed), 3)
    return {
        "doubles": noise(streams_of[0], (O, O, V, V), 1.0, 6.0, ((2, 8), (3, 16)), jnp.float32),
        "cycle_inter": noise(streams_of[1], (OV, OV), OV ** -0.5, 0.078125, ((0, 8), (1, 16)), jnp.float32),
    }


def reference(doubles, cycle_inter):
    amp_matrix = jnp.transpose(doubles, (0, 2, 1, 3)).reshape(O * V, O * V)
    return jnp.dot(cycle_inter, amp_matrix, precision=lax.Precision.HIGHEST, preferred_element_type=jnp.float32)
```

```python
import functools

import jax
import jax.numpy as jnp
import numpy as np
from jax import lax
from jax.experimental import pallas as pl
from jax.experimental.pallas import tpu as pltpu
from jax.sharding import PartitionSpec as P

MESH = pl.DeviceIdType.MESH
F32, BF16 = jnp.float32, jnp.bfloat16


def permutations():
    pack = np.zeros((2, 192, 384), np.float32)
    for half in range(2):
        for z in range(4):
            for core in range(2):
                for j2 in range(2):
                    for b in range(12):
                        j = 8 * z + 4 * half + 2 * core + j2
                        pack[half, ((z * 2 + core) * 2 + j2) * 12 + b, b * 32 + j] = 1
    unpack = np.zeros((384, 384), np.float32)
    for q in range(16):
        for j2 in range(2):
            for b in range(12):
                unpack[(q * 2 + j2) * 12 + b, j2 * 192 + q * 12 + b] = 1
    return pack, unpack


def halves(x):
    hi = x.astype(BF16)
    return hi, (x - hi.astype(F32)).astype(BF16)


def kernel(
    d_hbm, w_hbm, pack_hbm, unpack_hbm, out_ref,
    d, pack, unpack, x, t, r, amp, wb, whi, wlo, ahi, alo, acc, part,
    in_sem, a2a_s, a2a_r, x_s, x_r, y_s, y_r, f_s, f_r,
    w_s, w_r, g_s, g_r, n_s, n_r, c_s, c_r,
):
    row, col = lax.axis_index("row"), lax.axis_index("col")
    xh, y = row // 4, row % 4
    z, xl, core = col // 4, (col // 2) % 2, col % 2

    def dev(xh_, y_, z_, xl_, core_):
        return (xh_ * 4 + y_, z_ * 4 + xl_ * 2 + core_)

    ynext = (dev(xh, (y + 1) % 4, z, xl, core), dev(xh, (y + 3) % 4, z, xl, core))
    znext = (dev(xh, y, (z + 1) % 4, xl, core), dev(xh, y, (z + 3) % 4, xl, core))
    other_xh = dev(1 - xh, y, z, xl, core)
    other_xl = dev(xh, y, z, 1 - xl, core)
    twin = dev(xh, y, z, xl, 1 - core)

    loads = [
        pltpu.make_async_copy(d_hbm, d, in_sem.at[0]),
        pltpu.make_async_copy(pack_hbm, pack, in_sem.at[1]),
        pltpu.make_async_copy(unpack_hbm, unpack, in_sem.at[2]),
        pltpu.make_async_copy(w_hbm, wb.at[z, core], in_sem.at[3]),
    ]
    for load in loads:
        load.start()

    barrier = pltpu.get_barrier_semaphore()

    def greet(o, _):
        pl.semaphore_signal(barrier, inc=1, device_id=(row, (col + o) % 16), device_id_type=MESH)
        return 0

    lax.fori_loop(1, 16, greet, 0)
    for peer in ynext + (other_xh,):
        pl.semaphore_signal(barrier, inc=1, device_id=peer, device_id_type=MESH)
    pl.semaphore_wait(barrier, 18)

    def remote(src, dst, send, recv, to):
        return pltpu.make_async_remote_copy(
            src_ref=src, dst_ref=dst, send_sem=send, recv_sem=recv, device_id=to, device_id_type=MESH
        )

    def w_own(way, quarter):
        rows = pl.ds(quarter * 192, 192)
        return remote(w_hbm.at[rows], wb.at[z, core, rows], w_s.at[way, quarter], w_r.at[way, quarter], znext[way])

    def w_came(way, quarter):
        at = (z + 3) % 4 if way == 0 else (z + 1) % 4
        rows = pl.ds(quarter * 192, 192)
        return remote(wb.at[at, core, rows], wb.at[at, core, rows], w_s.at[way, quarter], w_r.at[way, quarter], znext[way])

    def w_pass(way):
        at = (z + 3) % 4 if way == 0 else (z + 1) % 4
        rows = pl.ds(way * 384, 384)
        return remote(wb.at[at, core, rows], wb.at[at, core, rows], g_s.at[way], g_r.at[way], znext[way])

    def w_passed(way):
        at = (z + 2) % 4
        rows = pl.ds(way * 384, 384)
        return remote(wb.at[at, core, rows], wb.at[at, core, rows], g_s.at[way], g_r.at[way], znext[way])

    def w_twin(off):
        at = (z + off) % 4
        src = w_hbm if off == 0 else wb.at[at, core]
        return remote(src, wb.at[at, core], n_s.at[off], n_r.at[off], twin)

    def w_twin_came(off):
        at = (z + off) % 4
        return remote(wb.at[at, 1 - core], wb.at[at, 1 - core], n_s.at[off], n_r.at[off], twin)

    def a2a(h, o):
        to = (col + o) % 16
        txl = (to // 2) % 2
        tz = (to // 4) * 2 + to % 2
        return remote(
            t.at[txl, (txl + 1 + h) % 2, tz], r.at[h, col], a2a_s.at[h, to], a2a_r.at[h, col], (row, to)
        )

    def a2a_came(h, o):
        src = (col + o) % 16
        return remote(r.at[h, src], r.at[h, src], a2a_s.at[h, src], a2a_r.at[h, src], (row, src))

    def send_a2a(h):
        def go(o, _):
            a2a(h, o).start()
            return 0

        lax.fori_loop(1, 16, go, 0)
        r[h, col] = t[xl, (xl + 1 + h) % 2, z * 2 + core]

    def unpack_half(h):
        def wait(o, _):
            a2a_came(h, o).wait_recv()
            return 0

        lax.fori_loop(1, 16, wait, 0)
        hi, lo = halves(jnp.transpose(r[h].reshape(384, 384)))
        block = jnp.dot(hi, unpack[...], preferred_element_type=F32)
        block += jnp.dot(lo, unpack[...], preferred_element_type=F32)
        amp[h, :, row] = block.reshape(16, 24, 384)

    def pack_half(lanes, half):
        hi, lo = halves(x[lanes].reshape(384, 384))
        nt = (((1,), (1,)), ((), ()))
        rows = lax.dot_general(pack[half], hi, nt, preferred_element_type=F32)
        rows += lax.dot_general(pack[half], lo, nt, preferred_element_type=F32)
        t[lanes, half] = rows.reshape(8, 24, 384)

    def place(s):
        p = s % 4
        return s // 4, (z + p + p // 2 - 2 * (p // 3)) % 4

    def slab(s, at, first=0, count=4):
        h, zz = place(s)
        return amp.at[h, pl.ds(zz * 4 + first, count), at]

    far = (1 - xh) * 4 + y

    def x_send(s):
        return remote(slab(s, row), slab(s, row), x_s.at[s], x_r.at[s], other_xh)

    def x_came(s):
        return remote(slab(s, far), slab(s, far), x_s.at[s], x_r.at[s], other_xh)

    def y_send(s, way, which):
        at = far if which else row
        return remote(slab(s, at), slab(s, at), y_s.at[s, way, which], y_r.at[s, way, which], ynext[way])

    def y_row(way, which, steps):
        at_xh = 1 - xh if which else xh
        return at_xh * 4 + (y + (4 - steps if way == 0 else steps)) % 4

    def y_came(s, way, which):
        at = y_row(way, which, 1)
        return remote(slab(s, at), slab(s, at), y_s.at[s, way, which], y_r.at[s, way, which], ynext[way])

    def f_send(s, way, which):
        at = y_row(way, which, 1)
        view = slab(s, at, 2 * way, 2)
        return remote(view, view, f_s.at[s, way, which], f_r.at[s, way, which], ynext[way])

    def f_came(s, way, which):
        at = y_row(way, which, 2)
        view = slab(s, at, 2 * way, 2)
        return remote(view, view, f_s.at[s, way, which], f_r.at[s, way, which], ynext[way])

    def split_w(zz):
        def block(m, _):
            rows = pl.ds(pl.multiple_of(m * 128, 128), 128)
            for c in range(2):
                hi, lo = halves(wb[zz, c, rows, :])
                whi[zz, rows, c * 384 : (c + 1) * 384] = hi
                wlo[zz, rows, c * 384 : (c + 1) * 384] = lo
            return 0

        lax.fori_loop(0, 6, block, 0)

    def compute(s):
        h, zz = place(s)

        @pl.when(s < 4)
        def _():
            split_w(zz)

        def split_a(k, _):
            hi, lo = halves(amp[h, zz * 4 + k].reshape(192, 384))
            rows = pl.ds(pl.multiple_of(k * 192, 64), 192)
            ahi[rows, :] = hi
            alo[rows, :] = lo
            return 0

        lax.fori_loop(0, 4, split_a, 0)

        def block(m, _):
            rows = pl.ds(pl.multiple_of(m * 256, 256), 256)
            a_hi, a_lo = ahi[...], alo[...]
            w_hi = whi[zz, rows, :]
            total = jnp.dot(w_hi, a_hi, preferred_element_type=F32)
            total += jnp.dot(w_hi, a_lo, preferred_element_type=F32)
            total += jnp.dot(wlo[zz, rows, :], a_hi, preferred_element_type=F32)
            acc[h, rows, :] += total
            return 0

        lax.fori_loop(0, 3, block, 0)

    def c_send():
        return remote(acc.at[0], part, c_s, c_r, other_xl)

    for way in range(2):
        w_own(way, 0).start()
    w_twin(0).start()
    acc[...] = jnp.zeros_like(acc)
    loads[0].wait()
    for lanes in range(2):
        for quad in range(3):
            for kk in range(16):
                k = 8 * (kk // 4) + 4 * lanes + kk % 4
                x[lanes, kk, :, quad * 128 : (quad + 1) * 128] = jnp.concatenate(
                    [d[k, quad * 4 + i] for i in range(4)], axis=-1
                )
    loads[1].wait()
    pack_half(0, 1)
    pack_half(1, 0)
    send_a2a(0)
    for way in range(2):
        for quarter in range(1, 4):
            w_own(way, quarter).start()
    pack_half(0, 0)
    pack_half(1, 1)
    send_a2a(1)
    loads[2].wait()
    unpack_half(0)

    def each_x(first):
        def go(s, _):
            x_send(s).start()
            return 0

        lax.fori_loop(first, first + 4, go, 0)

    each_x(0)
    for way in range(2):
        y_send(0, way, 0).start()
    x_came(0).wait_recv()
    for way in range(2):
        y_send(0, way, 1).start()
    loads[3].wait()

    def body(s, _):
        @pl.when(s < 7)
        def _():
            for way in range(2):
                y_send(s + 1, way, 0).start()
            x_came(s + 1).wait_recv()
            for way in range(2):
                y_send(s + 1, way, 1).start()

        for which in range(2):
            for way in range(2):
                y_came(s, way, which).wait_recv()
                f_send(s, way, which).start()

        @pl.when(s == 2)
        def _():
            for way in range(2):
                for quarter in range(4):
                    w_came(way, quarter).wait_recv()
                w_pass(way).start()
            w_twin(3).start()
            w_twin(1).start()
            w_twin_came(0).wait_recv()

        @pl.when(s == 3)
        def _():
            w_twin_came(1).wait_recv()
            w_twin_came(3).wait_recv()

        @pl.when(s == 4)
        def _():
            for way in range(2):
                w_passed(way).wait_recv()
            w_twin(2).start()

        @pl.when(s == 5)
        def _():
            w_twin_came(2).wait_recv()

        @pl.when(s >= 2)
        def _():
            compute(s - 2)

        @pl.when(s == 2)
        def _():
            unpack_half(1)
            each_x(4)

        @pl.when(s == 6)
        def _():
            c_send().start()

        @pl.when(s >= 1)
        def _():
            for which in range(2):
                for way in range(2):
                    f_came(s - 1, way, which).wait_recv()

        return 0

    lax.fori_loop(0, 8, body, 0)
    compute(6)
    for which in range(2):
        for way in range(2):
            f_came(7, way, which).wait_recv()
    compute(7)
    c_send().wait_recv()
    out_ref[...] = acc[1] + part[...]

    def drain_a2a(o, _):
        for h in range(2):
            a2a(h, o).wait_send()
        return 0

    lax.fori_loop(1, 16, drain_a2a, 0)

    def drain_y(s, _):
        x_send(s).wait_send()
        for which in range(2):
            for way in range(2):
                y_send(s, way, which).wait_send()
                f_send(s, way, which).wait_send()
        return 0

    lax.fori_loop(0, 8, drain_y, 0)
    for way in range(2):
        for quarter in range(4):
            w_own(way, quarter).wait_send()
        w_pass(way).wait_send()
    for off in range(4):
        w_twin(off).wait_send()
    c_send().wait_send()


def body(doubles, cycle_inter):
    pack, unpack = permutations()
    vmem, sems = pltpu.VMEM, pltpu.SemaphoreType.DMA
    return pl.pallas_call(
        kernel,
        out_shape=jax.ShapeDtypeStruct((768, 384), F32),
        in_specs=[pl.BlockSpec(memory_space=pl.ANY)] * 4,
        out_specs=pl.BlockSpec(memory_space=pltpu.VMEM),
        scratch_shapes=[
            vmem((32, 12, 24, 32), F32),
            vmem((2, 192, 384), BF16),
            vmem((384, 384), BF16),
            vmem((2, 16, 24, 384), F32),
            vmem((2, 2, 8, 24, 384), F32),
            vmem((2, 16, 24, 384), F32),
            vmem((2, 16, 8, 24, 384), F32),
            vmem((4, 2, 768, 384), F32),
            vmem((4, 768, 768), BF16),
            vmem((4, 768, 768), BF16),
            vmem((768, 384), BF16),
            vmem((768, 384), BF16),
            vmem((2, 768, 384), F32),
            vmem((768, 384), F32),
            sems((4,)),
            sems((2, 16)), sems((2, 16)),
            sems((8,)), sems((8,)),
            sems((8, 2, 2)), sems((8, 2, 2)),
            sems((8, 2, 2)), sems((8, 2, 2)),
            sems((2, 4)), sems((2, 4)),
            sems((2,)), sems((2,)),
            sems((4,)), sems((4,)),
            sems, sems,
        ],
        compiler_params=pltpu.CompilerParams(
            collective_id=1, has_side_effects=True, vmem_limit_bytes=62 * 1024 * 1024
        ),
        name="cycle_term",
    )(
        jnp.transpose(doubles, (0, 3, 2, 1)),
        cycle_inter,
        jnp.asarray(pack, BF16),
        jnp.asarray(unpack, BF16),
    )


def solution(mesh):
    return jax.shard_map(
        body,
        mesh=mesh,
        in_specs=(P(None, None, "row", "col"), P("row", "col")),
        out_specs=P("row", "col"),
        check_vma=False,
    )
```

```python
import functools

import jax
import jax.numpy as jnp
import numpy as np
from jax import lax
from jax.experimental import pallas as pl
from jax.experimental.pallas import tpu as pltpu
from jax.sharding import PartitionSpec as P

MESH = pl.DeviceIdType.MESH
F32, BF16 = jnp.float32, jnp.bfloat16


def permutations():
    pack = np.zeros((2, 192, 384), np.float32)
    for half in range(2):
        for z in range(4):
            for core in range(2):
                for j2 in range(2):
                    for b in range(12):
                        j = 8 * z + 4 * half + 2 * core + j2
                        pack[half, ((z * 2 + core) * 2 + j2) * 12 + b, b * 32 + j] = 1
    unpack = np.zeros((384, 384), np.float32)
    for q in range(16):
        for j2 in range(2):
            for b in range(12):
                unpack[(q * 2 + j2) * 12 + b, j2 * 192 + q * 12 + b] = 1
    return pack, unpack


def halves(x):
    hi = x.astype(BF16)
    return hi, (x - hi.astype(F32)).astype(BF16)


def kernel(
    d_hbm, w_hbm, pack_hbm, unpack_hbm, out_ref,
    d, pack, unpack, x, t, r, amp, wb, whi, wlo, ahi, alo, acc, part,
    in_sem, a2a_s, a2a_r, x_s, x_r, y_s, y_r, f_s, f_r,
    w_s, w_r, g_s, g_r, n_s, n_r, c_s, c_r,
):
    row, col = lax.axis_index("row"), lax.axis_index("col")
    xh, y = row // 4, row % 4
    z, xl, core = col // 4, (col // 2) % 2, col % 2

    def dev(xh_, y_, z_, xl_, core_):
        return (xh_ * 4 + y_, z_ * 4 + xl_ * 2 + core_)

    ynext = (dev(xh, (y + 1) % 4, z, xl, core), dev(xh, (y + 3) % 4, z, xl, core))
    znext = (dev(xh, y, (z + 1) % 4, xl, core), dev(xh, y, (z + 3) % 4, xl, core))
    other_xh = dev(1 - xh, y, z, xl, core)
    other_xl = dev(xh, y, z, 1 - xl, core)
    twin = dev(xh, y, z, xl, 1 - core)

    loads = [
        pltpu.make_async_copy(d_hbm, d, in_sem.at[0]),
        pltpu.make_async_copy(pack_hbm, pack, in_sem.at[1]),
        pltpu.make_async_copy(unpack_hbm, unpack, in_sem.at[2]),
        pltpu.make_async_copy(w_hbm, wb.at[z, core], in_sem.at[3]),
    ]
    for load in loads:
        load.start()

    barrier = pltpu.get_barrier_semaphore()

    def greet(o, _):
        pl.semaphore_signal(barrier, inc=1, device_id=(row, (col + o) % 16), device_id_type=MESH)
        return 0

    lax.fori_loop(1, 16, greet, 0)
    for peer in ynext + (other_xh,):
        pl.semaphore_signal(barrier, inc=1, device_id=peer, device_id_type=MESH)
    pl.semaphore_wait(barrier, 18)

    def remote(src, dst, send, recv, to):
        return pltpu.make_async_remote_copy(
            src_ref=src, dst_ref=dst, send_sem=send, recv_sem=recv, device_id=to, device_id_type=MESH
        )

    def w_own(way, quarter):
        rows = pl.ds(quarter * 192, 192)
        return remote(w_hbm.at[rows], wb.at[z, core, rows], w_s.at[way, quarter], w_r.at[way, quarter], znext[way])

    def w_came(way, quarter):
        at = (z + 3) % 4 if way == 0 else (z + 1) % 4
        rows = pl.ds(quarter * 192, 192)
        return remote(wb.at[at, core, rows], wb.at[at, core, rows], w_s.at[way, quarter], w_r.at[way, quarter], znext[way])

    def w_pass(way):
        at = (z + 3) % 4 if way == 0 else (z + 1) % 4
        rows = pl.ds(way * 384, 384)
        return remote(wb.at[at, core, rows], wb.at[at, core, rows], g_s.at[way], g_r.at[way], znext[way])

    def w_passed(way):
        at = (z + 2) % 4
        rows = pl.ds(way * 384, 384)
        return remote(wb.at[at, core, rows], wb.at[at, core, rows], g_s.at[way], g_r.at[way], znext[way])

    def w_twin(off):
        at = (z + off) % 4
        src = w_hbm if off == 0 else wb.at[at, core]
        return remote(src, wb.at[at, core], n_s.at[off], n_r.at[off], twin)

    def w_twin_came(off):
        at = (z + off) % 4
        return remote(wb.at[at, 1 - core], wb.at[at, 1 - core], n_s.at[off], n_r.at[off], twin)

    def a2a(h, o):
        to = (col + o) % 16
        txl = (to // 2) % 2
        tz = (to // 4) * 2 + to % 2
        return remote(
            t.at[txl, (txl + 1 + h) % 2, tz], r.at[h, col], a2a_s.at[h, to], a2a_r.at[h, col], (row, to)
        )

    def a2a_came(h, o):
        src = (col + o) % 16
        return remote(r.at[h, src], r.at[h, src], a2a_s.at[h, src], a2a_r.at[h, src], (row, src))

    def send_a2a(h):
        def go(o, _):
            a2a(h, o).start()
            return 0

        lax.fori_loop(1, 16, go, 0)
        r[h, col] = t[xl, (xl + 1 + h) % 2, z * 2 + core]

    def unpack_half(h):
        def wait(o, _):
            a2a_came(h, o).wait_recv()
            return 0

        lax.fori_loop(1, 16, wait, 0)
        hi, lo = halves(jnp.transpose(r[h].reshape(384, 384)))
        block = jnp.dot(hi, unpack[...], preferred_element_type=F32)
        block += jnp.dot(lo, unpack[...], preferred_element_type=F32)
        amp[h, :, row] = block.reshape(16, 24, 384)

    def pack_half(lanes, half):
        hi, lo = halves(x[lanes].reshape(384, 384))
        nt = (((1,), (1,)), ((), ()))
        rows = lax.dot_general(pack[half], hi, nt, preferred_element_type=F32)
        rows += lax.dot_general(pack[half], lo, nt, preferred_element_type=F32)
        t[lanes, half] = rows.reshape(8, 24, 384)

    def place(s):
        p = s % 4
        return s // 4, (z + p + p // 2 - 2 * (p // 3)) % 4

    def slab(s, at, first=0, count=4):
        h, zz = place(s)
        return amp.at[h, pl.ds(zz * 4 + first, count), at]

    far = (1 - xh) * 4 + y

    def x_send(s):
        return remote(slab(s, row), slab(s, row), x_s.at[s], x_r.at[s], other_xh)

    def x_came(s):
        return remote(slab(s, far), slab(s, far), x_s.at[s], x_r.at[s], other_xh)

    def y_send(s, way, which):
        at = far if which else row
        return remote(slab(s, at), slab(s, at), y_s.at[s, way, which], y_r.at[s, way, which], ynext[way])

    def y_row(way, which, steps):
        at_xh = 1 - xh if which else xh
        return at_xh * 4 + (y + (4 - steps if way == 0 else steps)) % 4

    def y_came(s, way, which):
        at = y_row(way, which, 1)
        return remote(slab(s, at), slab(s, at), y_s.at[s, way, which], y_r.at[s, way, which], ynext[way])

    def f_send(s, way, which):
        at = y_row(way, which, 1)
        view = slab(s, at, 2 * way, 2)
        return remote(view, view, f_s.at[s, way, which], f_r.at[s, way, which], ynext[way])

    def f_came(s, way, which):
        at = y_row(way, which, 2)
        view = slab(s, at, 2 * way, 2)
        return remote(view, view, f_s.at[s, way, which], f_r.at[s, way, which], ynext[way])

    def split_w(zz):
        def block(m, _):
            rows = pl.ds(pl.multiple_of(m * 128, 128), 128)
            for c in range(2):
                hi, lo = halves(wb[zz, c, rows, :])
                whi[zz, rows, c * 384 : (c + 1) * 384] = hi
                wlo[zz, rows, c * 384 : (c + 1) * 384] = lo
            return 0

        lax.fori_loop(0, 6, block, 0)

    def compute(s):
        h, zz = place(s)

        @pl.when(s < 4)
        def _():
            split_w(zz)

        def split_a(k, _):
            hi, lo = halves(amp[h, zz * 4 + k].reshape(192, 384))
            rows = pl.ds(pl.multiple_of(k * 192, 64), 192)
            ahi[rows, :] = hi
            alo[rows, :] = lo
            return 0

        lax.fori_loop(0, 4, split_a, 0)

        def block(m, _):
            rows = pl.ds(pl.multiple_of(m * 256, 256), 256)
            a_hi, a_lo = ahi[...], alo[...]
            w_hi = whi[zz, rows, :]
            total = jnp.dot(w_hi, a_hi, preferred_element_type=F32)
            total += jnp.dot(w_hi, a_lo, preferred_element_type=F32)
            total += jnp.dot(wlo[zz, rows, :], a_hi, preferred_element_type=F32)
            acc[h, rows, :] += total
            return 0

        lax.fori_loop(0, 3, block, 0)

    def c_send():
        return remote(acc.at[0], part, c_s, c_r, other_xl)

    for way in range(2):
        w_own(way, 0).start()
    w_twin(0).start()
    acc[...] = jnp.zeros_like(acc)
    loads[0].wait()
    for lanes in range(2):
        for quad in range(3):
            for kk in range(16):
                k = 8 * (kk // 4) + 4 * lanes + kk % 4
                x[lanes, kk, :, quad * 128 : (quad + 1) * 128] = jnp.concatenate(
                    [d[k, quad * 4 + i] for i in range(4)], axis=-1
                )
    loads[1].wait()
    pack_half(0, 1)
    pack_half(1, 0)
    send_a2a(0)
    for way in range(2):
        for quarter in range(1, 4):
            w_own(way, quarter).start()
    pack_half(0, 0)
    pack_half(1, 1)
    send_a2a(1)
    loads[2].wait()
    unpack_half(0)

    def each_x(first):
        def go(s, _):
            x_send(s).start()
            return 0

        lax.fori_loop(first, first + 4, go, 0)

    each_x(0)
    for way in range(2):
        y_send(0, way, 0).start()
    x_came(0).wait_recv()
    for way in range(2):
        y_send(0, way, 1).start()
    loads[3].wait()

    def body(s, _):
        @pl.when(s < 7)
        def _():
            for way in range(2):
                y_send(s + 1, way, 0).start()
            x_came(s + 1).wait_recv()
            for way in range(2):
                y_send(s + 1, way, 1).start()

        for which in range(2):
            for way in range(2):
                y_came(s, way, which).wait_recv()
                f_send(s, way, which).start()

        @pl.when(s == 2)
        def _():
            for way in range(2):
                for quarter in range(4):
                    w_came(way, quarter).wait_recv()
                w_pass(way).start()
            w_twin(3).start()
            w_twin(1).start()
            w_twin_came(0).wait_recv()

        @pl.when(s == 3)
        def _():
            w_twin_came(1).wait_recv()
            w_twin_came(3).wait_recv()

        @pl.when(s == 4)
        def _():
            for way in range(2):
                w_passed(way).wait_recv()
            w_twin(2).start()

        @pl.when(s == 5)
        def _():
            w_twin_came(2).wait_recv()

        @pl.when(s >= 2)
        def _():
            compute(s - 2)

        @pl.when(s == 2)
        def _():
            unpack_half(1)
            each_x(4)

        @pl.when(s == 5)
        def _():
            c_send().start()

        @pl.when(s >= 1)
        def _():
            for which in range(2):
                for way in range(2):
                    f_came(s - 1, way, which).wait_recv()

        return 0

    lax.fori_loop(0, 8, body, 0)
    compute(6)
    for which in range(2):
        for way in range(2):
            f_came(7, way, which).wait_recv()
    compute(7)
    c_send().wait_recv()
    out_ref[...] = acc[1] + part[...]

    def drain_a2a(o, _):
        for h in range(2):
            a2a(h, o).wait_send()
        return 0

    lax.fori_loop(1, 16, drain_a2a, 0)

    def drain_y(s, _):
        x_send(s).wait_send()
        for which in range(2):
            for way in range(2):
                y_send(s, way, which).wait_send()
                f_send(s, way, which).wait_send()
        return 0

    lax.fori_loop(0, 8, drain_y, 0)
    for way in range(2):
        for quarter in range(4):
            w_own(way, quarter).wait_send()
        w_pass(way).wait_send()
    for off in range(4):
        w_twin(off).wait_send()
    c_send().wait_send()


def body(doubles, cycle_inter):
    pack, unpack = permutations()
    vmem, sems = pltpu.VMEM, pltpu.SemaphoreType.DMA
    return pl.pallas_call(
        kernel,
        out_shape=jax.ShapeDtypeStruct((768, 384), F32),
        in_specs=[pl.BlockSpec(memory_space=pl.ANY)] * 4,
        out_specs=pl.BlockSpec(memory_space=pltpu.VMEM),
        scratch_shapes=[
            vmem((32, 12, 24, 32), F32),
            vmem((2, 192, 384), BF16),
            vmem((384, 384), BF16),
            vmem((2, 16, 24, 384), F32),
            vmem((2, 2, 8, 24, 384), F32),
            vmem((2, 16, 24, 384), F32),
            vmem((2, 16, 8, 24, 384), F32),
            vmem((4, 2, 768, 384), F32),
            vmem((4, 768, 768), BF16),
            vmem((4, 768, 768), BF16),
            vmem((768, 384), BF16),
            vmem((768, 384), BF16),
            vmem((2, 768, 384), F32),
            vmem((768, 384), F32),
            sems((4,)),
            sems((2, 16)), sems((2, 16)),
            sems((8,)), sems((8,)),
            sems((8, 2, 2)), sems((8, 2, 2)),
            sems((8, 2, 2)), sems((8, 2, 2)),
            sems((2, 4)), sems((2, 4)),
            sems((2,)), sems((2,)),
            sems((4,)), sems((4,)),
            sems, sems,
        ],
        compiler_params=pltpu.CompilerParams(
            collective_id=1, has_side_effects=True, vmem_limit_bytes=62 * 1024 * 1024
        ),
        name="cycle_term",
    )(
        jnp.transpose(doubles, (0, 3, 2, 1)),
        cycle_inter,
        jnp.asarray(pack, BF16),
        jnp.asarray(unpack, BF16),
    )


def solution(mesh):
    return jax.shard_map(
        body,
        mesh=mesh,
        in_specs=(P(None, None, "row", "col"), P("row", "col")),
        out_specs=P("row", "col"),
        check_vma=False,
    )
```

```python
import functools

import jax
import jax.numpy as jnp
import numpy as np
from jax import lax
from jax.experimental import pallas as pl
from jax.experimental.pallas import tpu as pltpu
from jax.sharding import PartitionSpec as P

MESH = pl.DeviceIdType.MESH
F32, BF16 = jnp.float32, jnp.bfloat16


def permutations():
    pack = np.zeros((2, 192, 384), np.float32)
    for half in range(2):
        for z in range(4):
            for core in range(2):
                for j2 in range(2):
                    for b in range(12):
                        j = 8 * z + 4 * half + 2 * core + j2
                        pack[half, ((z * 2 + core) * 2 + j2) * 12 + b, b * 32 + j] = 1
    unpack = np.zeros((384, 384), np.float32)
    for q in range(16):
        for j2 in range(2):
            for b in range(12):
                unpack[(q * 2 + j2) * 12 + b, j2 * 192 + q * 12 + b] = 1
    return pack, unpack


def halves(x):
    hi = x.astype(BF16)
    return hi, (x - hi.astype(F32)).astype(BF16)


def kernel(
    d_hbm, w_hbm, pack_hbm, unpack_hbm, out_ref,
    d, pack, unpack, x, t, r, amp, wb, whi, wlo, ahi, alo, acc, part,
    in_sem, a2a_s, a2a_r, x_s, x_r, y_s, y_r, f_s, f_r,
    w_s, w_r, g_s, g_r, n_s, n_r, c_s, c_r,
):
    row, col = lax.axis_index("row"), lax.axis_index("col")
    xh, y = row // 4, row % 4
    z, xl, core = col // 4, (col // 2) % 2, col % 2

    def dev(xh_, y_, z_, xl_, core_):
        return (xh_ * 4 + y_, z_ * 4 + xl_ * 2 + core_)

    ynext = (dev(xh, (y + 1) % 4, z, xl, core), dev(xh, (y + 3) % 4, z, xl, core))
    znext = (dev(xh, y, (z + 1) % 4, xl, core), dev(xh, y, (z + 3) % 4, xl, core))
    other_xh = dev(1 - xh, y, z, xl, core)
    other_xl = dev(xh, y, z, 1 - xl, core)
    twin = dev(xh, y, z, xl, 1 - core)

    barrier = pltpu.get_barrier_semaphore()

    def greet(o, _):
        pl.semaphore_signal(barrier, inc=1, device_id=(row, (col + o) % 16), device_id_type=MESH)
        return 0

    lax.fori_loop(1, 16, greet, 0)
    for peer in ynext + (other_xh,):
        pl.semaphore_signal(barrier, inc=1, device_id=peer, device_id_type=MESH)

    loads = [
        pltpu.make_async_copy(d_hbm, d, in_sem.at[0]),
        pltpu.make_async_copy(pack_hbm, pack, in_sem.at[1]),
        pltpu.make_async_copy(unpack_hbm, unpack, in_sem.at[2]),
        pltpu.make_async_copy(w_hbm, wb.at[z, core], in_sem.at[3]),
    ]
    for load in loads:
        load.start()

    def remote(src, dst, send, recv, to):
        return pltpu.make_async_remote_copy(
            src_ref=src, dst_ref=dst, send_sem=send, recv_sem=recv, device_id=to, device_id_type=MESH
        )

    def w_own(way, half):
        rows = pl.ds(half * 384, 384)
        return remote(w_hbm.at[rows], wb.at[z, core, rows], w_s.at[way, half], w_r.at[way, half], znext[way])

    def w_came(way, half):
        at = (z + 3) % 4 if way == 0 else (z + 1) % 4
        rows = pl.ds(half * 384, 384)
        return remote(wb.at[at, core, rows], wb.at[at, core, rows], w_s.at[way, half], w_r.at[way, half], znext[way])

    def w_pass(way):
        at = (z + 3) % 4 if way == 0 else (z + 1) % 4
        rows = pl.ds(way * 384, 384)
        return remote(wb.at[at, core, rows], wb.at[at, core, rows], g_s.at[way], g_r.at[way], znext[way])

    def w_passed(way):
        at = (z + 2) % 4
        rows = pl.ds(way * 384, 384)
        return remote(wb.at[at, core, rows], wb.at[at, core, rows], g_s.at[way], g_r.at[way], znext[way])

    def w_twin(off):
        at = (z + off) % 4
        src = w_hbm if off == 0 else wb.at[at, core]
        return remote(src, wb.at[at, core], n_s.at[off], n_r.at[off], twin)

    def w_twin_came(off):
        at = (z + off) % 4
        return remote(wb.at[at, 1 - core], wb.at[at, 1 - core], n_s.at[off], n_r.at[off], twin)

    def a2a(h, o):
        to = (col + o) % 16
        txl = (to // 2) % 2
        tz = (to // 4) * 2 + to % 2
        return remote(
            t.at[txl, (txl + 1 + h) % 2, tz], r.at[h, col], a2a_s.at[h, to], a2a_r.at[h, col], (row, to)
        )

    def a2a_came(h, o):
        src = (col + o) % 16
        return remote(r.at[h, src], r.at[h, src], a2a_s.at[h, src], a2a_r.at[h, src], (row, src))

    def send_a2a(h):
        def go(o, _):
            a2a(h, o).start()
            return 0

        lax.fori_loop(1, 16, go, 0)
        r[h, col] = t[xl, (xl + 1 + h) % 2, z * 2 + core]

    def unpack_half(h):
        def wait(o, _):
            a2a_came(h, o).wait_recv()
            return 0

        lax.fori_loop(1, 16, wait, 0)
        hi, lo = halves(jnp.transpose(r[h].reshape(384, 384)))
        block = jnp.dot(hi, unpack[...], preferred_element_type=F32)
        block += jnp.dot(lo, unpack[...], preferred_element_type=F32)
        amp[h, :, row] = block.reshape(16, 24, 384)

    def pack_half(lanes, half):
        hi, lo = halves(x[lanes].reshape(384, 384))
        nt = (((1,), (1,)), ((), ()))
        rows = lax.dot_general(pack[half], hi, nt, preferred_element_type=F32)
        rows += lax.dot_general(pack[half], lo, nt, preferred_element_type=F32)
        t[lanes, half] = rows.reshape(8, 24, 384)

    def place(s):
        p = s % 4
        return s // 4, (z + p + p // 2 - 2 * (p // 3)) % 4

    def slab(s, at, first=0, count=4):
        h, zz = place(s)
        return amp.at[h, pl.ds(zz * 4 + first, count), at]

    far = (1 - xh) * 4 + y

    def x_send(s):
        return remote(slab(s, row), slab(s, row), x_s.at[s], x_r.at[s], other_xh)

    def x_came(s):
        return remote(slab(s, far), slab(s, far), x_s.at[s], x_r.at[s], other_xh)

    def y_send(s, way, which):
        at = far if which else row
        return remote(slab(s, at), slab(s, at), y_s.at[s, way, which], y_r.at[s, way, which], ynext[way])

    def y_row(way, which, steps):
        at_xh = 1 - xh if which else xh
        return at_xh * 4 + (y + (4 - steps if way == 0 else steps)) % 4

    def y_came(s, way, which):
        at = y_row(way, which, 1)
        return remote(slab(s, at), slab(s, at), y_s.at[s, way, which], y_r.at[s, way, which], ynext[way])

    def f_send(s, way, which):
        at = y_row(way, which, 1)
        view = slab(s, at, 2 * way, 2)
        return remote(view, view, f_s.at[s, way, which], f_r.at[s, way, which], ynext[way])

    def f_came(s, way, which):
        at = y_row(way, which, 2)
        view = slab(s, at, 2 * way, 2)
        return remote(view, view, f_s.at[s, way, which], f_r.at[s, way, which], ynext[way])

    def split_w(zz):
        def block(m, _):
            rows = pl.ds(pl.multiple_of(m * 128, 128), 128)
            for c in range(2):
                hi, lo = halves(wb[zz, c, rows, :])
                whi[zz, rows, c * 384 : (c + 1) * 384] = hi
                wlo[zz, rows, c * 384 : (c + 1) * 384] = lo
            return 0

        lax.fori_loop(0, 6, block, 0)

    def compute(s):
        h, zz = place(s)

        @pl.when(s < 4)
        def _():
            split_w(zz)

        def split_a(k, _):
            hi, lo = halves(amp[h, zz * 4 + k].reshape(192, 384))
            rows = pl.ds(pl.multiple_of(k * 192, 64), 192)
            ahi[rows, :] = hi
            alo[rows, :] = lo
            return 0

        lax.fori_loop(0, 4, split_a, 0)

        def block(m, _):
            rows = pl.ds(pl.multiple_of(m * 256, 256), 256)
            a_hi, a_lo = ahi[...], alo[...]
            w_hi = whi[zz, rows, :]
            total = jnp.dot(w_hi, a_hi, preferred_element_type=F32)
            total += jnp.dot(w_hi, a_lo, preferred_element_type=F32)
            total += jnp.dot(wlo[zz, rows, :], a_hi, preferred_element_type=F32)
            acc[h, rows, :] += total
            return 0

        lax.fori_loop(0, 3, block, 0)

    def c_send():
        return remote(acc.at[0], part, c_s, c_r, other_xl)

    acc[...] = jnp.zeros_like(acc)
    loads[0].wait()
    for lanes in range(2):
        for quad in range(3):
            for kk in range(16):
                k = 8 * (kk // 4) + 4 * lanes + kk % 4
                x[lanes, kk, :, quad * 128 : (quad + 1) * 128] = jnp.concatenate(
                    [d[k, quad * 4 + i] for i in range(4)], axis=-1
                )
    loads[1].wait()
    for half in range(2):
        pack_half(0, half)
        pack_half(1, half)
    pl.semaphore_wait(barrier, 18)

    send_a2a(0)
    w_twin(0).start()
    for way in range(2):
        w_own(way, way).start()
    send_a2a(1)
    for way in range(2):
        w_own(way, 1 - way).start()
    loads[2].wait()
    unpack_half(0)

    def each_x(first):
        def go(s, _):
            x_send(s).start()
            return 0

        lax.fori_loop(first, first + 4, go, 0)

    def y_part(s):
        x_came(s).wait_recv()
        for way in range(2):
            y_send(s, way, 1).start()

    def y_own(s):
        for way in range(2):
            y_send(s, way, 0).start()

    def f_wait(s):
        for which in range(2):
            for way in range(2):
                f_came(s, way, which).wait_recv()

    each_x(0)
    y_own(0)
    y_own(1)
    y_part(0)
    loads[3].wait()

    def body(s, _):
        @pl.when(s == 3)
        def _():
            unpack_half(1)
            each_x(4)
            y_own(4)

        @pl.when(s < 7)
        def _():
            y_part(s + 1)

        for which in range(2):
            for way in range(2):
                y_came(s, way, which).wait_recv()
                f_send(s, way, which).start()

        @pl.when((s < 6) & (s != 2))
        def _():
            y_own(s + 2)

        @pl.when(s == 2)
        def _():
            w_twin_came(0).wait_recv()

        @pl.when(s == 3)
        def _():
            for way in range(2):
                for half in range(2):
                    w_came(way, half).wait_recv()
                w_pass(way).start()
            w_twin(3).start()
            w_twin(1).start()

        @pl.when(s == 4)
        def _():
            w_twin_came(1).wait_recv()
            w_twin_came(3).wait_recv()

            def two(n, _):
                compute(n)
                return 0

            lax.fori_loop(1, 3, two, 0)
            for way in range(2):
                w_passed(way).wait_recv()
            w_twin(2).start()

        @pl.when(s == 5)
        def _():
            w_twin_came(2).wait_recv()

        @pl.when((s == 2) | (s >= 5))
        def _():
            compute(s - 2)

        @pl.when(s == 5)
        def _():
            c_send().start()

        @pl.when(s >= 1)
        def _():
            f_wait(s - 1)

        return 0

    lax.fori_loop(0, 8, body, 0)
    compute(6)
    f_wait(7)
    compute(7)
    c_send().wait_recv()
    out_ref[...] = acc[1] + part[...]

    def drain_a2a(o, _):
        for h in range(2):
            a2a(h, o).wait_send()
        return 0

    lax.fori_loop(1, 16, drain_a2a, 0)

    def drain_y(s, _):
        x_send(s).wait_send()
        for which in range(2):
            for way in range(2):
                y_send(s, way, which).wait_send()
                f_send(s, way, which).wait_send()
        return 0

    lax.fori_loop(0, 8, drain_y, 0)
    for way in range(2):
        for half in range(2):
            w_own(way, half).wait_send()
        w_pass(way).wait_send()
    for off in range(4):
        w_twin(off).wait_send()
    c_send().wait_send()


def body(doubles, cycle_inter):
    pack, unpack = permutations()
    vmem, sems = pltpu.VMEM, pltpu.SemaphoreType.DMA
    return pl.pallas_call(
        kernel,
        out_shape=jax.ShapeDtypeStruct((768, 384), F32),
        in_specs=[pl.BlockSpec(memory_space=pl.ANY)] * 4,
        out_specs=pl.BlockSpec(memory_space=pltpu.VMEM),
        scratch_shapes=[
            vmem((32, 12, 24, 32), F32),
            vmem((2, 192, 384), BF16),
            vmem((384, 384), BF16),
            vmem((2, 16, 24, 384), F32),
            vmem((2, 2, 8, 24, 384), F32),
            vmem((2, 16, 24, 384), F32),
            vmem((2, 16, 8, 24, 384), F32),
            vmem((4, 2, 768, 384), F32),
            vmem((4, 768, 768), BF16),
            vmem((4, 768, 768), BF16),
            vmem((768, 384), BF16),
            vmem((768, 384), BF16),
            vmem((2, 768, 384), F32),
            vmem((768, 384), F32),
            sems((4,)),
            sems((2, 16)), sems((2, 16)),
            sems((8,)), sems((8,)),
            sems((8, 2, 2)), sems((8, 2, 2)),
            sems((8, 2, 2)), sems((8, 2, 2)),
            sems((2, 2)), sems((2, 2)),
            sems((2,)), sems((2,)),
            sems((4,)), sems((4,)),
            sems, sems,
        ],
        compiler_params=pltpu.CompilerParams(
            collective_id=1, has_side_effects=True, vmem_limit_bytes=62 * 1024 * 1024
        ),
        name="cycle_term",
    )(
        jnp.transpose(doubles, (0, 3, 2, 1)),
        cycle_inter,
        jnp.asarray(pack, BF16),
        jnp.asarray(unpack, BF16),
    )


def solution(mesh):
    return jax.shard_map(
        body,
        mesh=mesh,
        in_specs=(P(None, None, "row", "col"), P("row", "col")),
        out_specs=P("row", "col"),
        check_vma=False,
    )
```

```python
import functools

import jax
import jax.numpy as jnp
import numpy as np
from jax import lax
from jax.experimental import pallas as pl
from jax.experimental.pallas import tpu as pltpu
from jax.sharding import PartitionSpec as P

MESH = pl.DeviceIdType.MESH
F32, BF16 = jnp.float32, jnp.bfloat16


def permutations():
    pack = np.zeros((2, 192, 384), np.float32)
    for half in range(2):
        for z in range(4):
            for core in range(2):
                for j2 in range(2):
                    for b in range(12):
                        j = 8 * z + 4 * half + 2 * core + j2
                        pack[half, ((z * 2 + core) * 2 + j2) * 12 + b, b * 32 + j] = 1
    unpack = np.zeros((384, 384), np.float32)
    for q in range(16):
        for j2 in range(2):
            for b in range(12):
                unpack[(q * 2 + j2) * 12 + b, j2 * 192 + q * 12 + b] = 1
    return pack, unpack


def halves(x):
    hi = x.astype(BF16)
    return hi, (x - hi.astype(F32)).astype(BF16)


EARLY = 1


def kernel(
    d_hbm, w_hbm, pack_hbm, unpack_hbm, out_ref,
    d, pack, unpack, x, t, r, amp, wb, whi, wlo, ahi, alo, acc, part,
    in_sem, a2a_s, a2a_r, x_s, x_r, e_s, e_r, y_s, y_r, f_s, f_r,
    w_s, w_r, g_s, g_r, n_s, n_r, c_s, c_r,
):
    row, col = lax.axis_index("row"), lax.axis_index("col")
    xh, y = row >> 2, row & 3
    z, xl, core = col >> 2, (col >> 1) & 1, col & 1

    def dev(xh_, y_, z_, xl_, core_):
        return (xh_ * 4 + y_, z_ * 4 + xl_ * 2 + core_)

    ynext = (dev(xh, (y + 1) & 3, z, xl, core), dev(xh, (y + 3) & 3, z, xl, core))
    znext = (dev(xh, y, (z + 1) & 3, xl, core), dev(xh, y, (z + 3) & 3, xl, core))
    zfrom = ((z + 3) & 3, (z + 1) & 3)
    other_xh = dev(1 - xh, y, z, xl, core)
    other_xl = dev(xh, y, z, 1 - xl, core)
    twin = dev(xh, y, z, xl, 1 - core)

    barrier = pltpu.get_barrier_semaphore()

    def greet(o, _):
        pl.semaphore_signal(barrier, inc=1, device_id=(row, (col + o) & 15), device_id_type=MESH)
        return 0

    lax.fori_loop(1, 16, greet, 0)
    for peer in ynext + (other_xh,):
        pl.semaphore_signal(barrier, inc=1, device_id=peer, device_id_type=MESH)

    loads = [
        pltpu.make_async_copy(d_hbm, d, in_sem.at[0]),
        pltpu.make_async_copy(pack_hbm, pack, in_sem.at[1]),
        pltpu.make_async_copy(unpack_hbm, unpack, in_sem.at[2]),
        pltpu.make_async_copy(w_hbm, wb.at[z, core], in_sem.at[3]),
    ]
    for load in loads:
        load.start()

    def remote(src, dst, send, recv, to):
        return pltpu.make_async_remote_copy(
            src_ref=src, dst_ref=dst, send_sem=send, recv_sem=recv, device_id=to, device_id_type=MESH
        )

    W_ROWS = ((0, 384), (384, 192), (576, 192))

    def w_own(way, p):
        rows = pl.ds(*W_ROWS[p])
        return remote(w_hbm.at[rows], wb.at[z, core, rows], w_s.at[way, p], w_r.at[way, p], znext[way])

    def w_came(way, p):
        view = wb.at[zfrom[way], core, pl.ds(*W_ROWS[p])]
        return remote(view, view, w_s.at[way, p], w_r.at[way, p], znext[way])

    def w_pass(way, half, at):
        view = wb.at[at, core, pl.ds(half * 384 + way * 192, 192)]
        return remote(view, view, g_s.at[way, half], g_r.at[way, half], znext[way])

    def w_twin(off, half, plane, whole=False):
        view = wb.at[(z + off) & 3, plane] if whole else wb.at[(z + off) & 3, plane, pl.ds(half * 384, 384)]
        return remote(w_hbm if whole else view, view, n_s.at[off, half], n_r.at[off, half], twin)

    def order(z_, s):
        p = s & 3
        return (z_ + (p ^ (p >> 1))) & 3

    def a2a(s, o):
        to = (col + o) & 15
        txl = (to >> 1) & 1
        src = t.at[txl, (txl + 1 + (s >> 2)) & 1, order(to >> 2, s), ((to >> 2) << 1) | (to & 1)]
        return remote(src, r.at[s, col], a2a_s.at[s, to], a2a_r.at[s, col], (row, to))

    def a2a_came(s, o):
        src = (col + o) & 15
        return remote(r.at[s, src], r.at[s, src], a2a_s.at[s, src], a2a_r.at[s, src], (row, src))

    def send_a2a(s):
        def go(o, _):
            a2a(s, o).start()
            return 0

        lax.fori_loop(1, 16, go, 0)
        r[s, col] = t[xl, (xl + 1 + (s >> 2)) & 1, order(z, s), z * 2 + core]

    def unpack_step(s):
        def wait(o, _):
            a2a_came(s, o).wait_recv()
            return 0

        lax.fori_loop(1, 16, wait, 0)
        hi, lo = halves(jnp.transpose(r[s].reshape(384, 128))[:96])
        block = jnp.dot(hi, unpack[...], preferred_element_type=F32)
        block += jnp.dot(lo, unpack[...], preferred_element_type=F32)
        amp[s >> 2, pl.ds(order(z, s) * 4, 4), row] = block.reshape(4, 24, 384)

    def pack_half(lanes, half):
        hi, lo = halves(x[lanes].reshape(512, 384))
        nt = (((1,), (1,)), ((), ()))
        rows = lax.dot_general(pack[half], hi, nt, preferred_element_type=F32)
        rows += lax.dot_general(pack[half], lo, nt, preferred_element_type=F32)
        for zz in range(4):
            t[lanes, half, zz] = rows[:, zz * 128 : (zz + 1) * 128].reshape(8, 24, 128)

    def slab(s, at, first=0, count=4):
        return amp.at[s >> 2, pl.ds(order(z, s) * 4 + first, count), at]

    far = (1 - xh) * 4 + y

    def x_send(s):
        return remote(slab(s, row), slab(s, row), x_s.at[s], x_r.at[s], other_xh)

    def x_came(s):
        return remote(slab(s, far), slab(s, far), x_s.at[s], x_r.at[s], other_xh)

    def y_row(way, which, steps):
        at_xh = 1 - xh if which else xh
        return at_xh * 4 + ((y + (4 - steps if way == 0 else steps)) & 3)

    def y_send(s, way, which):
        at = far if which else row
        return remote(slab(s, at), slab(s, at), y_s.at[s, way, which], y_r.at[s, way, which], ynext[way])

    def y_came(s, way, which):
        at = y_row(way, which, 1)
        return remote(slab(s, at), slab(s, at), y_s.at[s, way, which], y_r.at[s, way, which], ynext[way])

    def f_copy(s, way, which, steps):
        view = slab(s, y_row(way, which, steps), 2 * way, 2)
        return remote(view, view, f_s.at[s, way, which], f_r.at[s, way, which], ynext[way])

    def e_near(way, which):
        view = slab(EARLY, y_row(way, which, 1))
        return remote(view, view, e_s.at[0, way], e_r.at[0, way], other_xh)

    def e_far(way, which):
        view = slab(EARLY, y_row(way, which, 2), 2 * way, 2)
        return remote(view, view, e_s.at[1, way], e_r.at[1, way], other_xh)

    def compute(u):
        late = u >> 3
        n = (1 - late) * (u & 3) + late * (u >> 1)
        rh = (1 - late) * ((u >> 2) & 1) + late * (u & 1)
        h, zz, slot = n >> 2, order(z, n), n & 3

        @pl.when(u < 8)
        def _():
            def split_w(m, _):
                rows = pl.ds(pl.multiple_of(rh * 384 + m * 128, 128), 128)
                for c in range(2):
                    hi, lo = halves(wb[zz, c, rows, :])
                    whi[zz, rows, c * 384 : (c + 1) * 384] = hi
                    wlo[zz, rows, c * 384 : (c + 1) * 384] = lo
                return 0

            lax.fori_loop(0, 3, split_w, 0)

        @pl.when(rh == 0)
        def _():
            def split_a(k, _):
                hi, lo = halves(amp[h, zz * 4 + k].reshape(192, 384))
                rows = pl.ds(pl.multiple_of(k * 192, 64), 192)
                ahi[slot, rows, :] = hi
                alo[slot, rows, :] = lo
                return 0

            lax.fori_loop(0, 4, split_a, 0)

        rows = pl.ds(pl.multiple_of(rh * 384, 128), 384)
        a_hi = ahi[slot]
        w_hi = whi[zz, rows, :]
        total = jnp.dot(w_hi, a_hi, preferred_element_type=F32)
        total += jnp.dot(w_hi, alo[slot], preferred_element_type=F32)
        total += jnp.dot(wlo[zz, rows, :], a_hi, preferred_element_type=F32)
        acc[h, rows, :] += total

    def units(first, last):
        def go(u, _):
            compute(u)
            return 0

        lax.fori_loop(first, last, go, 0)

    def c_send(half):
        rows = pl.ds(half * 384, 384)
        return remote(acc.at[0, rows], part.at[rows], c_s.at[half], c_r.at[half], other_xl)

    acc[...] = jnp.zeros_like(acc)
    x[:, :, 96:, :] = jnp.zeros((2, 4, 32, 384), F32)
    loads[0].wait()
    for lanes in range(2):
        for quad in range(3):
            for kk in range(16):
                k = 8 * (kk // 4) + 4 * lanes + kk % 4
                at = kk % 4 * 24
                x[lanes, kk // 4, at : at + 24, quad * 128 : (quad + 1) * 128] = jnp.concatenate(
                    [d[k, quad * 4 + i] for i in range(4)], axis=-1
                )
    loads[1].wait()
    for half in range(2):
        pack_half(0, half)
        pack_half(1, half)
    pl.semaphore_wait(barrier, 18)

    for s in range(4):
        send_a2a(s)
    loads[2].wait()

    def own(s):
        unpack_step(s)
        x_send(s).start()
        for way in range(2):
            y_send(s, way, 0).start()

    def beyond(s):
        x_came(s).wait_recv()
        for way in range(2):
            y_send(s, way, 1).start()

    def f_wait(s):
        for way in range(2):
            f_copy(s, way, 0, 2).wait_recv()

        @pl.when(s != EARLY)
        def _():
            for way in range(2):
                f_copy(s, way, 1, 2).wait_recv()

        @pl.when(s == EARLY)
        def _():
            for way in range(2):
                e_far(way, 0).start()

    own(0)
    own(1)
    beyond(0)
    send_a2a(4)
    for way in range(2):
        w_own(way, 0).start()
    w_twin(0, 0, core, True).start()
    loads[3].wait()

    def body(s, _):
        for way in range(2):
            y_came(s, way, 0).wait_recv()
            f_copy(s, way, 0, 1).start()

        @pl.when((s < 7) & (s + 1 != EARLY))
        def _():
            beyond(s + 1)

        @pl.when(s != EARLY)
        def _():
            for way in range(2):
                y_came(s, way, 1).wait_recv()
                f_copy(s, way, 1, 1).start()

        @pl.when(s < 5)
        def _():
            own(s + 2)

        @pl.when(s == EARLY)
        def _():
            for way in range(2):
                e_near(way, 0).start()

        @pl.when(s == 1)
        def _():
            send_a2a(5)

        @pl.when(s == 2)
        def _():
            for way in range(2):
                w_came(way, 0).wait_recv()
                w_pass(way, 0, zfrom[way]).start()
            send_a2a(6)
            for way in range(2):
                w_own(way, 1 + way).start()
            send_a2a(7)
            for way in range(2):
                w_own(way, 2 - way).start()
            for off in (1, 3):
                w_twin(off, 0, core).start()
            w_twin(0, 0, 1 - core, True).wait_recv()

        @pl.when(s == 3)
        def _():
            for way in range(2):
                w_pass(way, 0, (z + 2) & 3).wait_recv()
            w_twin(2, 0, core).start()
            for off in (1, 3):
                w_twin(off, 0, 1 - core).wait_recv()

        @pl.when(s == 4)
        def _():
            for way in range(2):
                w_came(way, 1 + way).wait_recv()
                w_pass(way, 1, zfrom[way]).start()
            w_twin(2, 0, 1 - core).wait_recv()

        @pl.when(s == 5)
        def _():
            for way in range(2):
                w_came(way, 2 - way).wait_recv()
            for off in (1, 3):
                w_twin(off, 1, core).start()
            for off in (1, 3):
                w_twin(off, 1, 1 - core).wait_recv()

        @pl.when(s == 6)
        def _():
            w_twin(2, 1, 1 - core).wait_recv()

        @pl.when(s == EARLY + 2)
        def _():
            x_came(EARLY).wait_recv()
            for way in range(2):
                e_near(way, 1).wait_recv()
                e_far(way, 1).wait_recv()

        @pl.when((s >= 2) & (s <= 4))
        def _():
            units(s - 2, s - 1)

        @pl.when(s >= 5)
        def _():
            units(4 + (s - 5) * 3, jnp.minimum(7 + (s - 5) * 3, 12))

        @pl.when(s == 6)
        def _():
            c_send(1).start()

        @pl.when(s >= 1)
        def _():
            f_wait(s - 1)

        @pl.when(s == 4)
        def _():
            own(7)
            units(3, 4)
            c_send(0).start()

        @pl.when(s == 5)
        def _():
            for way in range(2):
                w_pass(way, 1, (z + 2) & 3).wait_recv()
            w_twin(2, 1, core).start()

        return 0

    lax.fori_loop(0, 8, body, 0)
    units(12, 14)

    def drain(s, _):
        def each(o, _):
            a2a(s, o).wait_send()
            return 0

        lax.fori_loop(1, 16, each, 0)
        x_send(s).wait_send()
        for way in range(2):
            y_send(s, way, 0).wait_send()

        @pl.when(s != EARLY)
        def _():
            for way in range(2):
                y_send(s, way, 1).wait_send()

        return 0

    lax.fori_loop(0, 8, drain, 0)
    for way in range(2):
        e_near(way, 0).wait_send()
        e_far(way, 0).wait_send()
        for p in range(3):
            w_own(way, p).wait_send()
        for half in range(2):
            w_pass(way, half, zfrom[way]).wait_send()
    w_twin(0, 0, core, True).wait_send()
    for off in (1, 2, 3):
        for half in range(2):
            w_twin(off, half, core).wait_send()

    def f_drain(s, _):
        for way in range(2):
            f_copy(s, way, 0, 1).wait_send()

        @pl.when(s != EARLY)
        def _():
            for way in range(2):
                f_copy(s, way, 1, 1).wait_send()

        return 0

    lax.fori_loop(0, 7, f_drain, 0)
    for half in range(2):
        c_send(half).wait_recv()
    acc[1] += part[...]
    f_wait(7)
    units(14, 16)
    out_ref[...] = acc[1]
    f_drain(7, 0)
    for half in range(2):
        c_send(half).wait_send()


def body(doubles, cycle_inter):
    pack, unpack = permutations()
    vmem, sems = pltpu.VMEM, pltpu.SemaphoreType.DMA
    return pl.pallas_call(
        kernel,
        out_shape=jax.ShapeDtypeStruct((768, 384), F32),
        in_specs=[pl.BlockSpec(memory_space=pl.ANY)] * 4,
        out_specs=pl.BlockSpec(memory_space=pltpu.VMEM),
        scratch_shapes=[
            vmem((32, 12, 24, 32), F32),
            vmem((2, 192, 384), BF16),
            vmem((384, 384), BF16),
            vmem((2, 4, 128, 384), F32),
            vmem((2, 2, 4, 8, 24, 128), F32),
            vmem((8, 16, 24, 128), F32),
            vmem((2, 16, 8, 24, 384), F32),
            vmem((4, 2, 768, 384), F32),
            vmem((4, 768, 768), BF16),
            vmem((4, 768, 768), BF16),
            vmem((4, 768, 384), BF16),
            vmem((4, 768, 384), BF16),
            vmem((2, 768, 384), F32),
            vmem((768, 384), F32),
            sems((4,)),
            sems((8, 16)), sems((8, 16)),
            sems((8,)), sems((8,)),
            sems((2, 2)), sems((2, 2)),
            sems((8, 2, 2)), sems((8, 2, 2)),
            sems((8, 2, 2)), sems((8, 2, 2)),
            sems((2, 3)), sems((2, 3)),
            sems((2, 2)), sems((2, 2)),
            sems((4, 2)), sems((4, 2)),
            sems((2,)), sems((2,)),
        ],
        compiler_params=pltpu.CompilerParams(
            collective_id=1, has_side_effects=True, vmem_limit_bytes=62 * 1024 * 1024
        ),
        name="cycle_term",
    )(
        jnp.transpose(doubles, (0, 3, 2, 1)),
        cycle_inter,
        jnp.asarray(pack, BF16),
        jnp.asarray(unpack, BF16),
    )


def solution(mesh):
    return jax.shard_map(
        body,
        mesh=mesh,
        in_specs=(P(None, None, "row", "col"), P("row", "col")),
        out_specs=P("row", "col"),
        check_vma=False,
    )
```

```python
import functools

import jax
import jax.numpy as jnp
import numpy as np
from jax import lax
from jax.experimental import pallas as pl
from jax.experimental.pallas import tpu as pltpu
from jax.sharding import PartitionSpec as P

MESH = pl.DeviceIdType.MESH
F32, BF16 = jnp.float32, jnp.bfloat16


def permutations():
    pack = np.zeros((2, 192, 384), np.float32)
    for half in range(2):
        for z in range(4):
            for core in range(2):
                for j2 in range(2):
                    for b in range(12):
                        j = 8 * z + 4 * half + 2 * core + j2
                        pack[half, ((z * 2 + core) * 2 + j2) * 12 + b, b * 32 + j] = 1
    unpack = np.zeros((384, 384), np.float32)
    for q in range(16):
        for j2 in range(2):
            for b in range(12):
                unpack[(q * 2 + j2) * 12 + b, j2 * 192 + q * 12 + b] = 1
    return pack, unpack


def halves(x):
    hi = x.astype(BF16)
    return hi, (x - hi.astype(F32)).astype(BF16)


EARLY = 1


def kernel(
    d_hbm, w_hbm, pack_hbm, unpack_hbm, out_ref,
    d, pack, unpack, x, t, r, amp, wb, whi, wlo, ahi, alo, acc, part,
    in_sem, a2a_s, a2a_r, x_s, x_r, e_s, e_r, y_s, y_r, f_s, f_r,
    w_s, w_r, g_s, g_r, n_s, n_r, c_s, c_r,
):
    row, col = lax.axis_index("row"), lax.axis_index("col")
    xh, y = row >> 2, row & 3
    z, xl, core = col >> 2, (col >> 1) & 1, col & 1

    def dev(xh_, y_, z_, xl_, core_):
        return (xh_ * 4 + y_, z_ * 4 + xl_ * 2 + core_)

    ynext = (dev(xh, (y + 1) & 3, z, xl, core), dev(xh, (y + 3) & 3, z, xl, core))
    znext = (dev(xh, y, (z + 1) & 3, xl, core), dev(xh, y, (z + 3) & 3, xl, core))
    zfrom = ((z + 3) & 3, (z + 1) & 3)
    other_xh = dev(1 - xh, y, z, xl, core)
    other_xl = dev(xh, y, z, 1 - xl, core)
    twin = dev(xh, y, z, xl, 1 - core)

    barrier = pltpu.get_barrier_semaphore()

    def greet(o, _):
        pl.semaphore_signal(barrier, inc=1, device_id=(row, (col + o) & 15), device_id_type=MESH)
        return 0

    lax.fori_loop(1, 16, greet, 0)
    for peer in ynext + (other_xh,):
        pl.semaphore_signal(barrier, inc=1, device_id=peer, device_id_type=MESH)

    loads = [
        pltpu.make_async_copy(d_hbm, d, in_sem.at[0]),
        pltpu.make_async_copy(pack_hbm, pack, in_sem.at[1]),
        pltpu.make_async_copy(unpack_hbm, unpack, in_sem.at[2]),
        pltpu.make_async_copy(w_hbm, wb.at[z, core], in_sem.at[3]),
    ]
    for load in loads:
        load.start()

    def remote(src, dst, send, recv, to):
        return pltpu.make_async_remote_copy(
            src_ref=src, dst_ref=dst, send_sem=send, recv_sem=recv, device_id=to, device_id_type=MESH
        )

    W_ROWS = ((0, 384), (384, 192), (576, 192))

    def w_own(way, p):
        rows = pl.ds(*W_ROWS[p])
        return remote(w_hbm.at[rows], wb.at[z, core, rows], w_s.at[way, p], w_r.at[way, p], znext[way])

    def w_came(way, p):
        view = wb.at[zfrom[way], core, pl.ds(*W_ROWS[p])]
        return remote(view, view, w_s.at[way, p], w_r.at[way, p], znext[way])

    def w_pass(way, half, at):
        view = wb.at[at, core, pl.ds(half * 384 + way * 192, 192)]
        return remote(view, view, g_s.at[way, half], g_r.at[way, half], znext[way])

    def w_twin(off, half, plane, whole=False):
        view = wb.at[(z + off) & 3, plane] if whole else wb.at[(z + off) & 3, plane, pl.ds(half * 384, 384)]
        return remote(w_hbm if whole else view, view, n_s.at[off, half], n_r.at[off, half], twin)

    def order(z_, s):
        p = s & 3
        return (z_ + (p ^ (p >> 1))) & 3

    def a2a(s, o):
        to = (col + o) & 15
        txl = (to >> 1) & 1
        src = t.at[txl, (txl + 1 + (s >> 2)) & 1, order(to >> 2, s), ((to >> 2) << 1) | (to & 1)]
        return remote(src, r.at[s, col], a2a_s.at[s, to], a2a_r.at[s, col], (row, to))

    def a2a_came(s, o):
        src = (col + o) & 15
        return remote(r.at[s, src], r.at[s, src], a2a_s.at[s, src], a2a_r.at[s, src], (row, src))

    def send_a2a(s):
        def go(o, _):
            a2a(s, o).start()
            return 0

        lax.fori_loop(1, 16, go, 0)
        r[s, col] = t[xl, (xl + 1 + (s >> 2)) & 1, order(z, s), z * 2 + core]

    def unpack_step(s):
        def wait(o, _):
            a2a_came(s, o).wait_recv()
            return 0

        lax.fori_loop(1, 16, wait, 0)
        hi, lo = halves(jnp.transpose(r[s].reshape(384, 128))[:96])
        block = jnp.dot(hi, unpack[...], preferred_element_type=F32)
        block += jnp.dot(lo, unpack[...], preferred_element_type=F32)
        amp[s >> 2, pl.ds(order(z, s) * 4, 4), row] = block.reshape(4, 24, 384)

    def pack_half(lanes, half):
        hi, lo = halves(x[lanes].reshape(512, 384))
        nt = (((1,), (1,)), ((), ()))
        rows = lax.dot_general(pack[half], hi, nt, preferred_element_type=F32)
        rows += lax.dot_general(pack[half], lo, nt, preferred_element_type=F32)
        for zz in range(4):
            t[lanes, half, zz] = rows[:, zz * 128 : (zz + 1) * 128].reshape(8, 24, 128)

    def slab(s, at, first=0, count=4):
        return amp.at[s >> 2, pl.ds(order(z, s) * 4 + first, count), at]

    far = (1 - xh) * 4 + y

    def x_send(s):
        return remote(slab(s, row), slab(s, row), x_s.at[s], x_r.at[s], other_xh)

    def x_came(s):
        return remote(slab(s, far), slab(s, far), x_s.at[s], x_r.at[s], other_xh)

    def y_row(way, which, steps):
        at_xh = 1 - xh if which else xh
        return at_xh * 4 + ((y + (4 - steps if way == 0 else steps)) & 3)

    def y_send(s, way, which):
        at = far if which else row
        return remote(slab(s, at), slab(s, at), y_s.at[s, way, which], y_r.at[s, way, which], ynext[way])

    def y_came(s, way, which):
        at = y_row(way, which, 1)
        return remote(slab(s, at), slab(s, at), y_s.at[s, way, which], y_r.at[s, way, which], ynext[way])

    def f_copy(s, way, which, steps):
        view = slab(s, y_row(way, which, steps), 2 * way, 2)
        return remote(view, view, f_s.at[s, way, which], f_r.at[s, way, which], ynext[way])

    def e_near(way, which):
        view = slab(EARLY, y_row(way, which, 1))
        return remote(view, view, e_s.at[0, way], e_r.at[0, way], other_xh)

    def e_far(way, which):
        view = slab(EARLY, y_row(way, which, 2), 2 * way, 2)
        return remote(view, view, e_s.at[1, way], e_r.at[1, way], other_xh)

    def compute(u):
        late = u >> 3
        n = (1 - late) * (u & 3) + late * (u >> 1)
        rh = (1 - late) * ((u >> 2) & 1) + late * (u & 1)
        h, zz, slot = n >> 2, order(z, n), n & 3

        @pl.when(u < 8)
        def _():
            def split_w(m, _):
                rows = pl.ds(pl.multiple_of(rh * 384 + m * 128, 128), 128)
                for c in range(2):
                    hi, lo = halves(wb[zz, c, rows, :])
                    whi[zz, rows, c * 384 : (c + 1) * 384] = hi
                    wlo[zz, rows, c * 384 : (c + 1) * 384] = lo
                return 0

            lax.fori_loop(0, 3, split_w, 0)

        @pl.when(rh == 0)
        def _():
            def split_a(k, _):
                hi, lo = halves(amp[h, zz * 4 + k].reshape(192, 384))
                rows = pl.ds(pl.multiple_of(k * 192, 64), 192)
                ahi[slot, rows, :] = hi
                alo[slot, rows, :] = lo
                return 0

            lax.fori_loop(0, 4, split_a, 0)

        rows = pl.ds(pl.multiple_of(rh * 384, 128), 384)
        a_hi = ahi[slot]
        w_hi = whi[zz, rows, :]
        total = jnp.dot(w_hi, a_hi, preferred_element_type=F32)
        total += jnp.dot(w_hi, alo[slot], preferred_element_type=F32)
        total += jnp.dot(wlo[zz, rows, :], a_hi, preferred_element_type=F32)
        acc[h, rows, :] += total

    def units(first, last):
        def go(u, _):
            compute(u)
            return 0

        lax.fori_loop(first, last, go, 0)

    def c_send(half):
        rows = pl.ds(half * 384, 384)
        return remote(acc.at[0, rows], part.at[rows], c_s.at[half], c_r.at[half], other_xl)

    acc[...] = jnp.zeros_like(acc)
    x[:, :, 96:, :] = jnp.zeros((2, 4, 32, 384), F32)
    loads[0].wait()
    for lanes in range(2):
        for quad in range(3):
            for kk in range(16):
                k = 8 * (kk // 4) + 4 * lanes + kk % 4
                at = kk % 4 * 24
                x[lanes, kk // 4, at : at + 24, quad * 128 : (quad + 1) * 128] = jnp.concatenate(
                    [d[k, quad * 4 + i] for i in range(4)], axis=-1
                )
    loads[1].wait()
    for half in range(2):
        pack_half(0, half)
        pack_half(1, half)
    pl.semaphore_wait(barrier, 18)

    for s in range(4):
        send_a2a(s)
    loads[2].wait()

    def own(s):
        unpack_step(s)
        x_send(s).start()
        for way in range(2):
            y_send(s, way, 0).start()

    def beyond(s):
        x_came(s).wait_recv()
        for way in range(2):
            y_send(s, way, 1).start()

    def f_wait(s):
        for way in range(2):
            f_copy(s, way, 0, 2).wait_recv()

        @pl.when(s != EARLY)
        def _():
            for way in range(2):
                f_copy(s, way, 1, 2).wait_recv()

        @pl.when(s == EARLY)
        def _():
            for way in range(2):
                e_far(way, 0).start()

    own(0)
    own(1)
    beyond(0)
    send_a2a(4)
    for way in range(2):
        w_own(way, 0).start()
    w_twin(0, 0, core, True).start()
    loads[3].wait()

    def body(s, _):
        for way in range(2):
            y_came(s, way, 0).wait_recv()
            f_copy(s, way, 0, 1).start()

        @pl.when((s < 7) & (s + 1 != EARLY))
        def _():
            beyond(s + 1)

        @pl.when(s != EARLY)
        def _():
            for way in range(2):
                y_came(s, way, 1).wait_recv()
                f_copy(s, way, 1, 1).start()

        @pl.when(s < 5)
        def _():
            own(s + 2)

        @pl.when(s == EARLY)
        def _():
            for way in range(2):
                e_near(way, 0).start()

        @pl.when(s == 1)
        def _():
            send_a2a(5)

        @pl.when(s == 2)
        def _():
            for way in range(2):
                w_came(way, 0).wait_recv()
                w_pass(way, 0, zfrom[way]).start()
            send_a2a(6)
            for way in range(2):
                w_own(way, 1 + way).start()
            send_a2a(7)
            for way in range(2):
                w_own(way, 2 - way).start()
            for off in (1, 3):
                w_twin(off, 0, core).start()
            w_twin(0, 0, 1 - core, True).wait_recv()

        @pl.when(s == 3)
        def _():
            for way in range(2):
                w_pass(way, 0, (z + 2) & 3).wait_recv()
            w_twin(2, 0, core).start()
            for off in (1, 3):
                w_twin(off, 0, 1 - core).wait_recv()

        @pl.when(s == 4)
        def _():
            for way in range(2):
                w_came(way, 1 + way).wait_recv()
                w_pass(way, 1, zfrom[way]).start()
            w_twin(2, 0, 1 - core).wait_recv()

        @pl.when(s == 5)
        def _():
            for way in range(2):
                w_came(way, 2 - way).wait_recv()
            for off in (1, 3):
                w_twin(off, 1, core).start()
            for off in (1, 3):
                w_twin(off, 1, 1 - core).wait_recv()

        @pl.when(s == 6)
        def _():
            w_twin(2, 1, 1 - core).wait_recv()

        @pl.when(s == EARLY + 2)
        def _():
            x_came(EARLY).wait_recv()
            for way in range(2):
                e_near(way, 1).wait_recv()
                e_far(way, 1).wait_recv()

        @pl.when((s >= 2) & (s <= 4))
        def _():
            units(s - 2, s - 1)

        @pl.when(s >= 5)
        def _():
            units(4 + (s - 5) * 3, jnp.minimum(7 + (s - 5) * 3, 12))

        @pl.when(s == 6)
        def _():
            c_send(1).start()

        @pl.when(s >= 1)
        def _():
            f_wait(s - 1)

        @pl.when(s == 4)
        def _():
            own(7)
            units(3, 4)
            c_send(0).start()

        @pl.when(s == 5)
        def _():
            for way in range(2):
                w_pass(way, 1, (z + 2) & 3).wait_recv()
            w_twin(2, 1, core).start()

        return 0

    lax.fori_loop(0, 8, body, 0)
    units(12, 14)

    def drain(s, _):
        def each(o, _):
            a2a(s, o).wait_send()
            return 0

        lax.fori_loop(1, 16, each, 0)
        x_send(s).wait_send()
        for way in range(2):
            y_send(s, way, 0).wait_send()

        @pl.when(s != EARLY)
        def _():
            for way in range(2):
                y_send(s, way, 1).wait_send()

        return 0

    lax.fori_loop(0, 8, drain, 0)
    for way in range(2):
        e_near(way, 0).wait_send()
        e_far(way, 0).wait_send()
        for p in range(3):
            w_own(way, p).wait_send()
        for half in range(2):
            w_pass(way, half, zfrom[way]).wait_send()
    w_twin(0, 0, core, True).wait_send()
    for off in (1, 2, 3):
        for half in range(2):
            w_twin(off, half, core).wait_send()

    def f_drain(s, _):
        for way in range(2):
            f_copy(s, way, 0, 1).wait_send()

        @pl.when(s != EARLY)
        def _():
            for way in range(2):
                f_copy(s, way, 1, 1).wait_send()

        return 0

    lax.fori_loop(0, 7, f_drain, 0)
    for half in range(2):
        c_send(half).wait_recv()
    acc[1] += part[...]
    f_wait(7)
    outs = []
    for half in range(2):
        units(14 + half, 15 + half)
        rows = pl.ds(half * 384, 384)
        outs.append(pltpu.make_async_copy(acc.at[1, rows], out_ref.at[rows], in_sem.at[half]))
        outs[-1].start()
    for copy in outs:
        copy.wait()
    f_drain(7, 0)
    for half in range(2):
        c_send(half).wait_send()


def body(doubles, cycle_inter):
    pack, unpack = permutations()
    vmem, sems = pltpu.VMEM, pltpu.SemaphoreType.DMA
    return pl.pallas_call(
        kernel,
        out_shape=jax.ShapeDtypeStruct((768, 384), F32),
        in_specs=[pl.BlockSpec(memory_space=pl.ANY)] * 4,
        out_specs=pl.BlockSpec(memory_space=pl.ANY),
        scratch_shapes=[
            vmem((32, 12, 24, 32), F32),
            vmem((2, 192, 384), BF16),
            vmem((384, 384), BF16),
            vmem((2, 4, 128, 384), F32),
            vmem((2, 2, 4, 8, 24, 128), F32),
            vmem((8, 16, 24, 128), F32),
            vmem((2, 16, 8, 24, 384), F32),
            vmem((4, 2, 768, 384), F32),
            vmem((4, 768, 768), BF16),
            vmem((4, 768, 768), BF16),
            vmem((4, 768, 384), BF16),
            vmem((4, 768, 384), BF16),
            vmem((2, 768, 384), F32),
            vmem((768, 384), F32),
            sems((4,)),
            sems((8, 16)), sems((8, 16)),
            sems((8,)), sems((8,)),
            sems((2, 2)), sems((2, 2)),
            sems((8, 2, 2)), sems((8, 2, 2)),
            sems((8, 2, 2)), sems((8, 2, 2)),
            sems((2, 3)), sems((2, 3)),
            sems((2, 2)), sems((2, 2)),
            sems((4, 2)), sems((4, 2)),
            sems((2,)), sems((2,)),
        ],
        compiler_params=pltpu.CompilerParams(
            collective_id=1, has_side_effects=True, vmem_limit_bytes=64000000
        ),
        name="cycle_term",
    )(
        jnp.transpose(doubles, (0, 3, 2, 1)),
        cycle_inter,
        jnp.asarray(pack, BF16),
        jnp.asarray(unpack, BF16),
    )


def solution(mesh):
    return jax.shard_map(
        body,
        mesh=mesh,
        in_specs=(P(None, None, "row", "col"), P("row", "col")),
        out_specs=P("row", "col"),
        check_vma=False,
    )
```
